768 devices in a mesh: users: 48 (over z_hi, y, core), items: 16 (over x, z_lo).
Axes of the slice: x: 4, y: 8, z: 12 (z_hi: 3, z_lo: 4; z = z_hi * 4 + z_lo), core: 2. Of those that a mesh axis runs over, the one named last changes fastest.
Arguments:
- user_factors: float32 [98304, 128], P('users'), may hold values from -1.8 to 1.8
- user_moment_one: float32 [98304, 128], P('users'), may hold values from -1.8 to 1.8
- user_moment_two: float32 [98304, 128], P('users'), may hold values from 0.01 to 1
- item_factors: float32 [24576, 128], P(('items', 'users')), may hold values from -1.8 to 1.8
- item_moment_one: float32 [24576, 128], P(('items', 'users')), may hold values from -1.8 to 1.8
- item_moment_two: float32 [24576, 128], P(('items', 'users')), may hold values from 0.01 to 1
- block_slot: int32 [48, 16, 128], P('users', 'items'), may hold values from 0 to 191, as said below
- block_count: int32 [48, 16], P('users', 'items'), may hold values from 32 to 128, as said below
- block_values: bfloat16 [48, 16, 128, 128, 128], P('users', 'items'), may hold values from 0 to 4
Outputs:
- new_user_factors: float32 [98304, 128], P(('users', 'items'))
- new_user_moment_one: float32 [98304, 128], P(('users', 'items'))
- new_user_moment_two: float32 [98304, 128], P(('users', 'items'))
- new_item_factors: float32 [24576, 128], P(('items', 'users'))
- new_item_moment_one: float32 [24576, 128], P(('items', 'users'))
- new_item_moment_two: float32 [24576, 128], P(('items', 'users'))
The draws below stay inside these ranges and needn't reach their ends.
Inputs may be any that keep to these rules, and one draw needn't show every extreme that they name: `block_slot`: in every grid cell the 128 entries are distinct. `block_count`: some grid cell has exactly 128 live blocks.
All inputs are finite; a program needn't handle non-finite values.
Results may differ from the reference program's by a relative error of at most 0.0046.
Values may be sent and summed in bfloat16 or wider, within the bound.
No kernel may reach another device: no remote copies, remote signals or barrier semaphores. Data moves between devices by JAX's collectives and lax.ppermute only.
A program may use at most 64 MiB of HBM per device.

```python
import math
import jax
import jax.numpy as jnp
from jax import lax

R = 128
BS = 128
UBLK = 16
IBLK = 12
MAXB = 128
GRID_ROWS = 48
GRID_COLS = 16
NU = 98304
NI = 24576


def draw_block_slot(key, part):
    cell_keys = jax.random.split(jax.random.fold_in(key, 11), GRID_ROWS * GRID_COLS)
    orderings = jax.vmap(lambda single: jax.random.permutation(single, UBLK * IBLK)[:MAXB])(cell_keys)
    return orderings.reshape(GRID_ROWS, GRID_COLS, MAXB).astype(jnp.int32)


def draw_block_count(key, part):
    cell_total = GRID_ROWS * GRID_COLS
    divider = jax.random.randint(jax.random.fold_in(key, 23), (cell_total,), 1, 5)
    counts = MAXB // divider
    chosen = jax.random.randint(jax.random.fold_in(key, 29), (), 0, cell_total)
    counts = jnp.where(jnp.arange(cell_total) == chosen, MAXB, counts)
    return counts.reshape(GRID_ROWS, GRID_COLS).astype(jnp.int32)


def levels(rng, extent, pieces, smallest, top_value):
    def one(position, shards_of):
        steps = jax.random.uniform(jax.random.fold_in(jax.random.fold_in(rng, 6), position), (shards_of,), jnp.float32, smallest / len(pieces), top_value / len(pieces))
        return jnp.repeat(jnp.exp(steps), extent[position] // shards_of).reshape((-1,) + (1,) * (len(extent) - position - 1))

    loudness = one(*pieces[0])
    for cut in pieces[1:]:
        loudness = loudness * one(*cut)
    return loudness


def noise(key, extent, width, bound, cuts=(), held_as=jnp.bfloat16):
    drawn = width * jax.random.normal(key, extent, jnp.float32)
    if cuts:
        drawn = drawn * levels(key, extent, cuts, -0.22, 0.18)
    return jnp.clip(drawn, -bound, bound).astype(held_as)


def setup_inputs(seed: int = 0) -> dict:
    keys = jax.random.split(jax.random.key(seed), 10)
    return {
        "user_factors": noise(keys[0], (NU, R), 0.3, 1.8, ((0, 48),), jnp.float32),
        "user_moment_one": noise(keys[1], (NU, R), 0.3, 1.8, ((0, 48),), jnp.float32),
        "user_moment_two": jnp.clip(jnp.exp(math.log(1.0) - 4.6051702 * jax.random.uniform(keys[2], (NU, R), jnp.float32) ** levels(keys[2], (NU, R), ((0, 48),), -0.2, 0.2)), 0.01, 1.0),
        "item_factors": noise(keys[3], (NI, R), 0.3, 1.8, ((0, 768),), jnp.float32),
        "item_moment_one": noise(keys[4], (NI, R), 0.3, 1.8, ((0, 768),), jnp.float32),
        "item_moment_two": jnp.clip(jnp.exp(math.log(1.0) - 4.6051702 * jax.random.uniform(keys[5], (NI, R), jnp.float32) ** levels(keys[5], (NI, R), ((0, 768),), -0.2, 0.2)), 0.01, 1.0),
        "block_slot": draw_block_slot(jax.random.fold_in(keys[9], 71), 0),
        "block_count": draw_block_count(jax.random.fold_in(keys[9], 71), 0),
        "block_values": jnp.clip(4.0 * jax.random.uniform(keys[8], (GRID_ROWS, GRID_COLS, MAXB, BS, BS), jnp.float32) ** levels(keys[8], (GRID_ROWS, GRID_COLS, MAXB, BS, BS), ((0, 48), (1, 16)), -0.2, 0.2), 0.0, 4.0).astype(jnp.bfloat16),
    }


conf_alpha = 0.5
reg_weight = 0.5
beta_one = 0.9
beta_two = 0.95
learn_rate = 0.1
adam_eps = 1e-08
correction_one = 1.0 - beta_one ** 11
correction_two = 1.0 - beta_two ** 11

def adam_update(parameter, first_moment, second_moment, grad_sum, grad_scale):
    gradient = grad_sum * grad_scale + reg_weight * parameter
    first_new = beta_one * first_moment + (1.0 - beta_one) * gradient
    second_new = beta_two * second_moment + (1.0 - beta_two) * gradient * gradient
    step_size = first_new / correction_one / (jnp.sqrt(second_new / correction_two) + adam_eps)
    return (parameter - learn_rate * step_size, first_new, second_new)

def weighted_error(predicted, block_vals, live_mask):
    target = block_vals.astype(jnp.float32)
    return jnp.where(live_mask, (1.0 + conf_alpha * target) * (predicted - target), 0.0).astype(jnp.bfloat16)

def cell_error(user_tiles, item_tiles, block_slot, block_count, block_values, row_index, col_index):
    slot_list = block_slot[row_index, col_index]
    live_mask = jnp.arange(MAXB, dtype=jnp.int32) < block_count[row_index, col_index]
    user_part = (slot_list // IBLK).astype(jnp.int32)
    item_part = (slot_list % IBLK).astype(jnp.int32)
    user_rows = user_tiles[row_index][user_part].astype(jnp.float32)
    item_rows = item_tiles[col_index][item_part].astype(jnp.float32)
    predicted = jnp.einsum('kar,kbr->kab', user_rows, item_rows)
    weighted = weighted_error(predicted, block_values[row_index, col_index], live_mask[:, None, None])
    weighted = lax.optimization_barrier(weighted).astype(jnp.float32)
    return (weighted, user_part, item_part, user_rows, item_rows)

def user_pass(user_low, item_low, block_slot, block_count, block_values):
    user_tiles = lax.optimization_barrier(user_low).reshape(GRID_ROWS, UBLK, BS, R)
    item_tiles = lax.optimization_barrier(item_low).reshape(GRID_COLS, IBLK, BS, R)

    def one_row(row_index):

        def one_cell(running, col_index):
            weighted, user_part, item_part, user_rows, item_rows = cell_error(user_tiles, item_tiles, block_slot, block_count, block_values, row_index, col_index)
            running = running.at[user_part].add(jnp.einsum('kab,kbr->kar', weighted, item_rows))
            return (running, None)
        running, _ = lax.scan(one_cell, jnp.zeros((UBLK, BS, R), jnp.float32), jnp.arange(GRID_COLS, dtype=jnp.int32))
        return running
    return lax.map(one_row, jnp.arange(GRID_ROWS, dtype=jnp.int32)).reshape(NU, R)

def item_pass(user_low, item_low, block_slot, block_count, block_values):
    user_tiles = lax.optimization_barrier(user_low).reshape(GRID_ROWS, UBLK, BS, R)
    item_tiles = lax.optimization_barrier(item_low).reshape(GRID_COLS, IBLK, BS, R)

    def one_col(col_index):

        def one_cell(running, row_index):
            weighted, user_part, item_part, user_rows, item_rows = cell_error(user_tiles, item_tiles, block_slot, block_count, block_values, row_index, col_index)
            running = running.at[item_part].add(jnp.einsum('kab,kar->kbr', weighted, user_rows))
            return (running, None)
        running, _ = lax.scan(one_cell, jnp.zeros((IBLK, BS, R), jnp.float32), jnp.arange(GRID_ROWS, dtype=jnp.int32))
        return running
    return lax.map(one_col, jnp.arange(GRID_COLS, dtype=jnp.int32)).reshape(NI, R)

def reference(user_factors, user_moment_one, user_moment_two, item_factors, item_moment_one, item_moment_two, block_slot, block_count, block_values):
    item_low = item_factors.astype(jnp.bfloat16)
    user_low = user_factors.astype(jnp.bfloat16)
    user_sum = user_pass(user_low, item_low, block_slot, block_count, block_values)
    new_user, new_user_one, new_user_two = adam_update(user_factors, user_moment_one, user_moment_two, user_sum, 1.0 / math.sqrt(NI))
    new_user_low = new_user.astype(jnp.bfloat16)
    item_sum = item_pass(new_user_low, item_low, block_slot, block_count, block_values)
    new_item, new_item_one, new_item_two = adam_update(item_factors, item_moment_one, item_moment_two, item_sum, 1.0 / math.sqrt(NU))
    return (new_user, new_user_one, new_user_two, new_item, new_item_one, new_item_two)
```

```python
import functools
import math

import jax
import jax.numpy as jnp
from jax import lax
from jax.experimental import pallas as pl
from jax.experimental.pallas import tpu as pltpu
from jax.sharding import Mesh
from jax.sharding import PartitionSpec as P

conf_alpha = 0.5
reg_weight = 0.5
beta_one = 0.9
beta_two = 0.95
learn_rate = 0.1
adam_eps = 1e-08
correction_one = 1.0 - beta_one**11
correction_two = 1.0 - beta_two**11

EDGE = 128
RANK = 128
UBLK = 16
IBLK = 12
MAXB = 128
CHUNK = 8
PARTS = ("z_hi", "y", "core", "x", "z_lo")
USERS = PARTS[:3]
ITEMS = PARTS[3:]


def adam_update(parameter, first_moment, second_moment, grad_sum, grad_scale):
    gradient = grad_sum * grad_scale + reg_weight * parameter
    first_new = beta_one * first_moment + (1.0 - beta_one) * gradient
    second_new = beta_two * second_moment + (1.0 - beta_two) * gradient * gradient
    step_size = first_new / correction_one / (jnp.sqrt(second_new / correction_two) + adam_eps)
    return (parameter - learn_rate * step_size, first_new, second_new)


def dot_nt(left, right):
    return lax.dot_general(
        left, right, (((1,), (1,)), ((), ())), preferred_element_type=jnp.float32
    )


def dot_nn(left, right):
    return lax.dot_general(
        left, right, (((1,), (0,)), ((), ())), preferred_element_type=jnp.float32
    )


def load_values(count, values, buffer, arrivals):
    for chunk in range(MAXB // CHUNK):

        @pl.when(chunk * CHUNK < count)
        def _():
            pltpu.make_async_copy(
                values.at[pl.ds(chunk * CHUNK, CHUNK)],
                buffer.at[pl.ds(chunk * CHUNK, CHUNK)],
                arrivals.at[chunk],
            ).start()


def await_values(count, values, buffer, arrivals):
    for chunk in range(MAXB // CHUNK):

        @pl.when(chunk * CHUNK < count)
        def _():
            pltpu.make_async_copy(
                values.at[pl.ds(chunk * CHUNK, CHUNK)],
                buffer.at[pl.ds(chunk * CHUNK, CHUNK)],
                arrivals.at[chunk],
            ).wait()


def fill_places(count, slots, places):
    for place in range(UBLK * IBLK):
        places[place] = MAXB

    def advance(turn, carry):
        for inner in range(CHUNK):
            listed = turn * CHUNK + inner
            place = slots[listed]
            places[place] = jnp.where(listed < count, listed, places[place])
        return carry

    lax.fori_loop(0, (count + CHUNK - 1) // CHUNK, advance, 0)


def weighted(predicted, target):
    target = target.astype(jnp.float32)
    return ((1.0 + conf_alpha * target) * (predicted - target)).astype(jnp.bfloat16)


def square_error(user_pair, item_pair, first_place, places, buffer):
    predicted = dot_nt(user_pair, item_pair)
    rows = []
    for row in range(2):
        columns = []
        for column in range(2):
            block = buffer[places[first_place + row * IBLK + column]]
            columns.append(
                weighted(
                    predicted[row * EDGE : (row + 1) * EDGE, column * EDGE : (column + 1) * EDGE],
                    block,
                )
            )
        rows.append(jnp.concatenate(columns, axis=1))
    return jnp.concatenate(rows, axis=0)


def user_kernel(slots, count, users, items, values, out, places_out, buffer, places, arrivals):
    live = count[0]
    load_values(live, values, buffer, arrivals)
    buffer[MAXB] = jnp.full((EDGE, EDGE), -2.0, jnp.bfloat16)
    fill_places(live, slots, places)
    await_values(live, values, buffer, arrivals)

    def advance(pair, carry):
        rows = pl.ds(pl.multiple_of(pair * 2 * EDGE, 2 * EDGE), 2 * EDGE)
        user_pair = users[rows, :].astype(jnp.bfloat16)
        running = jnp.zeros((2 * EDGE, RANK), jnp.float32)
        for turn in range(IBLK // 2):
            item_pair = items[turn * 2 * EDGE : (turn + 1) * 2 * EDGE, :]
            error = square_error(
                user_pair, item_pair, pair * 2 * IBLK + turn * 2, places, buffer
            )
            running = running + dot_nn(error, item_pair)
        out[rows, :] = running.astype(jnp.bfloat16)
        return carry

    lax.fori_loop(0, UBLK // 2, advance, 0)
    for place in range(UBLK * IBLK):
        places_out[place] = places[place]


def item_kernel(count, places, users, items, values, out, buffer, turned, arrivals):
    live = count[0]
    load_values(live, values, buffer, arrivals)
    buffer[MAXB] = jnp.full((EDGE, EDGE), -2.0, jnp.bfloat16)
    for block in range(UBLK):
        turned[:, block * EDGE : (block + 1) * EDGE] = users[
            block * EDGE : (block + 1) * EDGE, :
        ].T
    await_values(live, values, buffer, arrivals)

    def advance(turn, carry):
        rows = pl.ds(pl.multiple_of(turn * 2 * EDGE, 2 * EDGE), 2 * EDGE)
        item_pair = items[rows, :]
        running = jnp.zeros((RANK, 2 * EDGE), jnp.float32)
        for pair in range(UBLK // 2):
            span = slice(pair * 2 * EDGE, (pair + 1) * 2 * EDGE)
            error = square_error(
                users[span, :], item_pair, pair * 2 * IBLK + turn * 2, places, buffer
            )
            running = running + dot_nn(turned[:, span], error)
        out[rows, :] = running.T.astype(jnp.bfloat16)
        return carry

    lax.fori_loop(0, IBLK // 2, advance, 0)


def whole(space):
    return pl.BlockSpec(memory_space=space)


def user_pass(slots, count, users, items, values):
    return pl.pallas_call(
        user_kernel,
        out_shape=(
            jax.ShapeDtypeStruct((UBLK * EDGE, RANK), jnp.bfloat16),
            jax.ShapeDtypeStruct((UBLK * IBLK,), jnp.int32),
        ),
        in_specs=[
            whole(pltpu.SMEM),
            whole(pltpu.SMEM),
            whole(pltpu.VMEM),
            whole(pltpu.VMEM),
            whole(pl.ANY),
        ],
        out_specs=(whole(pltpu.VMEM), whole(pltpu.SMEM)),
        scratch_shapes=[
            pltpu.VMEM((MAXB + 1, EDGE, EDGE), jnp.bfloat16),
            pltpu.SMEM((UBLK * IBLK,), jnp.int32),
            pltpu.SemaphoreType.DMA((MAXB // CHUNK,)),
        ],
        name="user_pass",
    )(slots, count, users, items, values)


def item_pass(count, places, users, items, values):
    return pl.pallas_call(
        item_kernel,
        out_shape=jax.ShapeDtypeStruct((IBLK * EDGE, RANK), jnp.bfloat16),
        in_specs=[
            whole(pltpu.SMEM),
            whole(pltpu.SMEM),
            whole(pltpu.VMEM),
            whole(pltpu.VMEM),
            whole(pl.ANY),
        ],
        out_specs=whole(pltpu.VMEM),
        scratch_shapes=[
            pltpu.VMEM((MAXB + 1, EDGE, EDGE), jnp.bfloat16),
            pltpu.VMEM((RANK, UBLK * EDGE), jnp.bfloat16),
            pltpu.SemaphoreType.DMA((MAXB // CHUNK,)),
        ],
        name="item_pass",
    )(count, places, users, items, values)


def on_device(
    user_factors,
    user_moment_one,
    user_moment_two,
    item_factors,
    item_moment_one,
    item_moment_two,
    block_slot,
    block_count,
    block_values,
):
    slots = block_slot.reshape(MAXB)
    count = block_count.reshape(1)
    values = block_values.reshape(MAXB, EDGE, EDGE)
    item_total = IBLK * EDGE * lax.axis_size(ITEMS)
    user_total = user_factors.shape[0] * lax.axis_size(USERS)
    items = lax.all_gather(item_factors.astype(jnp.bfloat16), USERS, axis=0, tiled=True)
    user_partial, places = user_pass(slots, count, user_factors, items, values)
    user_share = user_factors.shape[0] // lax.axis_size(ITEMS)
    user_offset = lax.axis_index(ITEMS) * user_share
    sent = user_partial.reshape(-1, user_share, RANK)
    got = lax.all_to_all(sent, ITEMS, 0, 0)
    user_sum = jnp.sum(got.astype(jnp.float32), axis=0)
    mine = functools.partial(
        lax.dynamic_slice_in_dim, start_index=user_offset, slice_size=user_share, axis=0
    )
    new_user, new_user_one, new_user_two = adam_update(
        mine(user_factors),
        mine(user_moment_one),
        mine(user_moment_two),
        user_sum,
        1.0 / math.sqrt(item_total),
    )
    new_low = lax.all_gather(new_user.astype(jnp.bfloat16), ITEMS, axis=0, tiled=True)
    item_partial = item_pass(count, places, new_low, items, values)
    item_share = item_factors.shape[0]
    sent = item_partial.reshape(-1, item_share, RANK)
    got = lax.all_to_all(sent, USERS, 0, 0)
    item_sum = jnp.sum(got.astype(jnp.float32), axis=0)
    new_item, new_item_one, new_item_two = adam_update(
        item_factors, item_moment_one, item_moment_two, item_sum, 1.0 / math.sqrt(user_total)
    )
    return (new_user, new_user_one, new_user_two, new_item, new_item_one, new_item_two)


def solution(mesh):
    fine = Mesh(mesh.devices.reshape(3, 8, 2, 4, 4), PARTS)
    return jax.shard_map(
        on_device,
        mesh=fine,
        in_specs=(
            P(USERS, None),
            P(USERS, None),
            P(USERS, None),
            P(ITEMS + USERS, None),
            P(ITEMS + USERS, None),
            P(ITEMS + USERS, None),
            P(USERS, ITEMS, None),
            P(USERS, ITEMS),
            P(USERS, ITEMS, None, None, None),
        ),
        out_specs=(
            P(USERS + ITEMS, None),
            P(USERS + ITEMS, None),
            P(USERS + ITEMS, None),
            P(ITEMS + USERS, None),
            P(ITEMS + USERS, None),
            P(ITEMS + USERS, None),
        ),
        check_vma=False,
    )
```

```python
import functools
import math

import jax
import jax.numpy as jnp
from jax import lax
from jax.experimental import pallas as pl
from jax.experimental.pallas import tpu as pltpu
from jax.sharding import Mesh
from jax.sharding import PartitionSpec as P

conf_alpha = 0.5
reg_weight = 0.5
beta_one = 0.9
beta_two = 0.95
learn_rate = 0.1
adam_eps = 1e-08
correction_one = 1.0 - beta_one**11
correction_two = 1.0 - beta_two**11

EDGE = 128
RANK = 128
UBLK = 16
IBLK = 12
MAXB = 128
CHUNK = 8
PARTS = ("z_hi", "y", "core", "x", "z_lo")
USERS = PARTS[:3]
ITEMS = PARTS[3:]


def adam_update(parameter, first_moment, second_moment, grad_sum, grad_scale):
    gradient = grad_sum * grad_scale + reg_weight * parameter
    first_new = beta_one * first_moment + (1.0 - beta_one) * gradient
    second_new = beta_two * second_moment + (1.0 - beta_two) * gradient * gradient
    step_size = first_new / correction_one / (jnp.sqrt(second_new / correction_two) + adam_eps)
    return (parameter - learn_rate * step_size, first_new, second_new)


def dot_nt(left, right):
    return lax.dot_general(
        left, right, (((1,), (1,)), ((), ())), preferred_element_type=jnp.float32
    )


def dot_nn(left, right):
    return lax.dot_general(
        left, right, (((1,), (0,)), ((), ())), preferred_element_type=jnp.float32
    )


def fill_places(count, slots, places):
    for place in range(UBLK * IBLK):
        places[place] = MAXB

    def advance(turn, carry):
        for inner in range(CHUNK):
            listed = turn * CHUNK + inner
            place = slots[listed]
            places[place] = jnp.where(listed < count, listed, places[place])
        return carry

    lax.fori_loop(0, (count + CHUNK - 1) // CHUNK, advance, 0)


def value_copies(values, buffer, arrivals):
    return [
        pltpu.make_async_copy(
            values.at[pl.ds(chunk * CHUNK, CHUNK)],
            buffer.at[pl.ds(chunk * CHUNK, CHUNK)],
            arrivals.at[chunk],
        )
        for chunk in range(MAXB // CHUNK)
    ]


def weighted(predicted, place, values):
    live = place < MAXB
    base = jnp.where(live, 1.0, 0.0).astype(jnp.float32)
    slope = jnp.where(live, conf_alpha, 0.0).astype(jnp.float32)
    target = values[jnp.minimum(place, MAXB - 1)].astype(jnp.float32)
    return ((base + slope * target) * (predicted - target)).astype(jnp.bfloat16)


def square_error(user_pair, item_pair, first_place, places, values):
    predicted = dot_nt(user_pair, item_pair)
    rows = []
    for row in range(2):
        columns = []
        for column in range(2):
            part = predicted[row * EDGE : (row + 1) * EDGE, column * EDGE : (column + 1) * EDGE]
            columns.append(weighted(part, places[first_place + row * IBLK + column], values))
        rows.append(jnp.concatenate(columns, axis=1))
    return jnp.concatenate(rows, axis=0)


def user_kernel(
    slots, count, users, gathered, values, out, panel, places_out, places, low, buffer, arrivals, ready
):
    copies = value_copies(values, buffer, arrivals)
    fetch = pltpu.make_async_copy(users, low, ready)
    fetch.start()
    for copy in copies:
        copy.start()
    fill_places(count[0], slots, places)
    share = gathered.shape[2]
    for rank in range(gathered.shape[1]):
        for core in range(2):
            first = (rank * 2 + core) * share
            panel[first : first + share, :] = gathered[core, rank]
    for place in range(UBLK * IBLK):
        places_out[place] = places[place]
    fetch.wait()
    for copy in copies:
        copy.wait()

    def advance(pair, carry):
        rows = pl.ds(pl.multiple_of(pair * 2 * EDGE, 2 * EDGE), 2 * EDGE)
        user_pair = low[rows, :].astype(jnp.bfloat16)
        running = jnp.zeros((2 * EDGE, RANK), jnp.float32)
        for turn in range(IBLK // 2):
            item_pair = panel[turn * 2 * EDGE : (turn + 1) * 2 * EDGE, :]
            error = square_error(
                user_pair, item_pair, pair * 2 * IBLK + turn * 2, places, buffer
            )
            running = running + dot_nn(error, item_pair)
        out[rows, :] = running.astype(jnp.bfloat16)
        return carry

    lax.fori_loop(0, UBLK // 2, advance, 0)


def item_kernel(core, places, users, items, values, keep, sent, turned, buffer, arrivals):
    copies = value_copies(values, buffer, arrivals)
    for copy in copies:
        copy.start()
    for block in range(UBLK):
        turned[:, block * EDGE : (block + 1) * EDGE] = users[
            block * EDGE : (block + 1) * EDGE, :
        ].T
    share = keep.shape[1]
    ranks = EDGE // share
    first_core = core[0] == 0
    for copy in copies:
        copy.wait()

    def advance(turn, carry):
        rows = pl.ds(pl.multiple_of(turn * 2 * EDGE, 2 * EDGE), 2 * EDGE)
        item_pair = items[rows, :]
        running = jnp.zeros((RANK, 2 * EDGE), jnp.float32)
        for pair in range(UBLK // 2):
            span = slice(pair * 2 * EDGE, (pair + 1) * 2 * EDGE)
            error = square_error(
                users[span, :], item_pair, pair * 2 * IBLK + turn * 2, places, buffer
            )
            running = running + dot_nn(turned[:, span], error)
        split = running.T.reshape(ranks, 2, share, RANK)
        even, odd = split[:, 0], split[:, 1]
        where = pl.ds(turn * ranks, ranks)
        keep[where] = jnp.where(first_core, even, odd)
        sent[where] = jnp.where(first_core, odd, even).astype(jnp.bfloat16)
        return carry

    lax.fori_loop(0, IBLK // 2, advance, 0)


def whole(space):
    return pl.BlockSpec(memory_space=space)


def user_pass(slots, count, users, gathered, values):
    panel = (gathered.shape[0] * gathered.shape[1] * gathered.shape[2], RANK)
    return pl.pallas_call(
        user_kernel,
        out_shape=(
            jax.ShapeDtypeStruct((UBLK * EDGE, RANK), jnp.bfloat16),
            jax.ShapeDtypeStruct(panel, jnp.bfloat16),
            jax.ShapeDtypeStruct((UBLK * IBLK,), jnp.int32),
        ),
        in_specs=[
            whole(pltpu.SMEM),
            whole(pltpu.SMEM),
            whole(pltpu.HBM),
            whole(pltpu.VMEM),
            whole(pltpu.HBM),
        ],
        out_specs=(whole(pltpu.VMEM), whole(pltpu.VMEM), whole(pltpu.SMEM)),
        scratch_shapes=[
            pltpu.SMEM((UBLK * IBLK,), jnp.int32),
            pltpu.VMEM((UBLK * EDGE, RANK), jnp.float32),
            pltpu.VMEM((MAXB, EDGE, EDGE), jnp.bfloat16),
            pltpu.SemaphoreType.DMA((MAXB // CHUNK,)),
            pltpu.SemaphoreType.DMA,
        ],
        name="user_pass",
    )(slots, count, users, gathered, values)


def item_pass(core, places, users, items, values, share):
    ranks = items.shape[0] // (2 * share)
    return pl.pallas_call(
        item_kernel,
        out_shape=(
            jax.ShapeDtypeStruct((ranks, share, RANK), jnp.float32),
            jax.ShapeDtypeStruct((ranks, share, RANK), jnp.bfloat16),
        ),
        in_specs=[
            whole(pltpu.SMEM),
            whole(pltpu.SMEM),
            whole(pltpu.VMEM),
            whole(pltpu.VMEM),
            whole(pltpu.HBM),
        ],
        out_specs=(whole(pltpu.VMEM), whole(pltpu.VMEM)),
        scratch_shapes=[
            pltpu.VMEM((RANK, UBLK * EDGE), jnp.bfloat16),
            pltpu.VMEM((MAXB, EDGE, EDGE), jnp.bfloat16),
            pltpu.SemaphoreType.DMA((MAXB // CHUNK,)),
        ],
        name="item_pass",
    )(core, places, users, items, values)


def spread(mine, axes):
    ranks = lax.axis_size(axes)
    return lax.all_to_all(jnp.broadcast_to(mine[None], (ranks,) + mine.shape), axes, 0, 0)


def on_device(
    user_factors,
    user_moment_one,
    user_moment_two,
    item_factors,
    item_moment_one,
    item_moment_two,
    block_slot,
    block_count,
    block_values,
):
    slots = block_slot.reshape(MAXB)
    count = block_count.reshape(1)
    values = block_values.reshape(MAXB, EDGE, EDGE)
    item_total = IBLK * EDGE * lax.axis_size(ITEMS)
    user_total = user_factors.shape[0] * lax.axis_size(USERS)
    half = spread(item_factors.astype(jnp.bfloat16), ("z_hi", "y"))
    gathered = lax.all_gather(half, "core", axis=0)
    user_partial, items, places = user_pass(slots, count, user_factors, gathered, values)
    user_share = user_factors.shape[0] // lax.axis_size(ITEMS)
    user_offset = lax.axis_index(ITEMS) * user_share
    sent = user_partial.reshape(-1, user_share, RANK)
    got = lax.all_to_all(sent, ITEMS, 0, 0)
    user_sum = jnp.sum(got.astype(jnp.float32), axis=0)
    mine = functools.partial(
        lax.dynamic_slice_in_dim, start_index=user_offset, slice_size=user_share, axis=0
    )
    new_user, new_user_one, new_user_two = adam_update(
        mine(user_factors),
        mine(user_moment_one),
        mine(user_moment_two),
        user_sum,
        1.0 / math.sqrt(item_total),
    )
    new_low = spread(new_user.astype(jnp.bfloat16), ITEMS).reshape(-1, RANK)
    core = lax.axis_index("core").reshape(1)
    keep, sent = item_pass(core, places, new_low, items, values, item_factors.shape[0])
    other = lax.ppermute(sent, "core", [(0, 1), (1, 0)])
    both = (keep + other.astype(jnp.float32)).astype(jnp.bfloat16)
    got = lax.all_to_all(both, ("z_hi", "y"), 0, 0)
    item_sum = jnp.sum(got.astype(jnp.float32), axis=0)
    new_item, new_item_one, new_item_two = adam_update(
        item_factors, item_moment_one, item_moment_two, item_sum, 1.0 / math.sqrt(user_total)
    )
    return (new_user, new_user_one, new_user_two, new_item, new_item_one, new_item_two)


def solution(mesh):
    fine = Mesh(mesh.devices.reshape(3, 8, 2, 4, 4), PARTS)
    return jax.shard_map(
        on_device,
        mesh=fine,
        in_specs=(
            P(USERS, None),
            P(USERS, None),
            P(USERS, None),
            P(ITEMS + USERS, None),
            P(ITEMS + USERS, None),
            P(ITEMS + USERS, None),
            P(USERS, ITEMS, None),
            P(USERS, ITEMS),
            P(USERS, ITEMS, None, None, None),
        ),
        out_specs=(
            P(USERS + ITEMS, None),
            P(USERS + ITEMS, None),
            P(USERS + ITEMS, None),
            P(ITEMS + USERS, None),
            P(ITEMS + USERS, None),
            P(ITEMS + USERS, None),
        ),
        check_vma=False,
    )
```

```python
import functools
import math

import jax
import jax.numpy as jnp
from jax import lax
from jax.experimental import pallas as pl
from jax.experimental.pallas import tpu as pltpu
from jax.sharding import Mesh
from jax.sharding import PartitionSpec as P

conf_alpha = 0.5
reg_weight = 0.5
beta_one = 0.9
beta_two = 0.95
learn_rate = 0.1
adam_eps = 1e-08
correction_one = 1.0 - beta_one**11
correction_two = 1.0 - beta_two**11

EDGE = 128
RANK = 128
UBLK = 16
IBLK = 12
MAXB = 128
CHUNK = 8
PARTS = ("z_hi", "y", "core", "x", "z_lo")
USERS = PARTS[:3]
ITEMS = PARTS[3:]


def adam_update(parameter, first_moment, second_moment, grad_sum, grad_scale):
    gradient = grad_sum * grad_scale + reg_weight * parameter
    first_new = beta_one * first_moment + (1.0 - beta_one) * gradient
    second_new = beta_two * second_moment + (1.0 - beta_two) * gradient * gradient
    step_size = first_new / correction_one / (jnp.sqrt(second_new / correction_two) + adam_eps)
    return (parameter - learn_rate * step_size, first_new, second_new)


def dot_nt(left, right):
    return lax.dot_general(
        left, right, (((1,), (1,)), ((), ())), preferred_element_type=jnp.float32
    )


def dot_nn(left, right):
    return lax.dot_general(
        left, right, (((1,), (0,)), ((), ())), preferred_element_type=jnp.float32
    )


def fill_places(count, slots, places):
    for place in range(UBLK * IBLK):
        places[place] = MAXB

    def advance(turn, carry):
        for inner in range(CHUNK):
            listed = turn * CHUNK + inner
            place = slots[listed]
            places[place] = jnp.where(listed < count, listed, places[place])
        return carry

    lax.fori_loop(0, (count + CHUNK - 1) // CHUNK, advance, 0)


def value_copies(values, buffer, arrivals):
    return [
        pltpu.make_async_copy(
            values.at[pl.ds(chunk * CHUNK, CHUNK)],
            buffer.at[pl.ds(chunk * CHUNK, CHUNK)],
            arrivals.at[chunk],
        )
        for chunk in range(MAXB // CHUNK)
    ]


def weighted(predicted, place, values):
    live = place < MAXB
    base = jnp.where(live, 1.0, 0.0).astype(jnp.float32)
    slope = jnp.where(live, conf_alpha, 0.0).astype(jnp.float32)
    target = values[jnp.minimum(place, MAXB - 1)].astype(jnp.float32)
    return ((base + slope * target) * (predicted - target)).astype(jnp.bfloat16)


def square_error(user_pair, item_pair, first_place, places, values):
    predicted = dot_nt(user_pair, item_pair)
    rows = []
    for row in range(2):
        columns = []
        for column in range(2):
            part = predicted[row * EDGE : (row + 1) * EDGE, column * EDGE : (column + 1) * EDGE]
            columns.append(weighted(part, places[first_place + row * IBLK + column], values))
        rows.append(jnp.concatenate(columns, axis=1))
    return jnp.concatenate(rows, axis=0)


def user_kernel(
    slots, count, users, gathered, values, out, panel, places_out, places, low, buffer, arrivals, ready
):
    copies = value_copies(values, buffer, arrivals)
    fetch = pltpu.make_async_copy(users, low, ready)
    fetch.start()
    for copy in copies:
        copy.start()
    fill_places(count[0], slots, places)
    share = gathered.shape[2]
    for rank in range(gathered.shape[1]):
        for core in range(2):
            first = (rank * 2 + core) * share
            panel[first : first + share, :] = gathered[core, rank]
    for place in range(UBLK * IBLK):
        places_out[place] = places[place]
    fetch.wait()
    for copy in copies:
        copy.wait()

    def advance(pair, carry):
        rows = pl.ds(pl.multiple_of(pair * 2 * EDGE, 2 * EDGE), 2 * EDGE)
        user_pair = low[rows, :].astype(jnp.bfloat16)
        errors = []
        for turn in range(IBLK // 2):
            item_pair = panel[turn * 2 * EDGE : (turn + 1) * 2 * EDGE, :]
            errors.append(
                square_error(user_pair, item_pair, pair * 2 * IBLK + turn * 2, places, buffer)
            )
        total = dot_nn(jnp.concatenate(errors, axis=1), panel[...])
        out[rows, :] = total.astype(jnp.bfloat16)
        return carry

    lax.fori_loop(0, UBLK // 2, advance, 0, unroll=4)


def item_kernel(core, places, users, items, values, keep, sent, turned, buffer, arrivals):
    copies = value_copies(values, buffer, arrivals)
    for copy in copies:
        copy.start()
    for block in range(UBLK):
        turned[:, block * EDGE : (block + 1) * EDGE] = users[
            block * EDGE : (block + 1) * EDGE, :
        ].T
    share = keep.shape[1]
    ranks = EDGE // share
    first_core = core[0] == 0
    for copy in copies:
        copy.wait()

    def advance(turn, carry):
        rows = pl.ds(pl.multiple_of(turn * 2 * EDGE, 2 * EDGE), 2 * EDGE)
        item_pair = items[rows, :]
        errors = []
        for pair in range(UBLK // 2):
            span = slice(pair * 2 * EDGE, (pair + 1) * 2 * EDGE)
            errors.append(
                square_error(users[span, :], item_pair, pair * 2 * IBLK + turn * 2, places, buffer)
            )
        running = dot_nn(turned[...], jnp.concatenate(errors, axis=0))
        split = running.T.reshape(ranks, 2, share, RANK)
        even, odd = split[:, 0], split[:, 1]
        where = pl.ds(turn * ranks, ranks)
        keep[where] = jnp.where(first_core, even, odd)
        sent[where] = jnp.where(first_core, odd, even).astype(jnp.bfloat16)
        return carry

    lax.fori_loop(0, IBLK // 2, advance, 0, unroll=3)


def user_update_kernel(
    offset, got, parameter, first, second, new, new_first, new_second, shared, mine, arrivals, scale
):
    rows = pl.ds(pl.multiple_of(offset[0], EDGE), EDGE)
    copies = [
        pltpu.make_async_copy(source.at[rows], mine.at[place], arrivals.at[place])
        for place, source in enumerate((parameter, first, second))
    ]
    for copy in copies:
        copy.start()
    total = got[0].astype(jnp.float32)
    for rank in range(1, got.shape[0]):
        total = total + got[rank].astype(jnp.float32)
    for copy in copies:
        copy.wait()
    updated = adam_update(mine[0], mine[1], mine[2], total, scale)
    new[...], new_first[...], new_second[...] = updated
    low = updated[0].astype(jnp.bfloat16)
    for rank in range(got.shape[0]):
        shared[rank] = low


def share_kernel(items, shared):
    low = items[...].astype(jnp.bfloat16)
    for rank in range(shared.shape[0]):
        shared[rank] = low


def whole(space):
    return pl.BlockSpec(memory_space=space)


def grant(mebibytes):
    return pltpu.CompilerParams(vmem_limit_bytes=mebibytes * 1024 * 1024)


def share_items(items, ranks):
    return pl.pallas_call(
        share_kernel,
        out_shape=jax.ShapeDtypeStruct((ranks,) + items.shape, jnp.bfloat16),
        in_specs=[whole(pltpu.VMEM)],
        out_specs=whole(pltpu.VMEM),
        name="share_items",
    )(items)


def user_pass(slots, count, users, gathered, values):
    panel = (gathered.shape[0] * gathered.shape[1] * gathered.shape[2], RANK)
    return pl.pallas_call(
        user_kernel,
        out_shape=(
            jax.ShapeDtypeStruct((UBLK * EDGE, RANK), jnp.bfloat16),
            jax.ShapeDtypeStruct(panel, jnp.bfloat16),
            jax.ShapeDtypeStruct((UBLK * IBLK,), jnp.int32),
        ),
        in_specs=[
            whole(pltpu.SMEM),
            whole(pltpu.SMEM),
            whole(pltpu.HBM),
            whole(pltpu.VMEM),
            whole(pltpu.HBM),
        ],
        out_specs=(whole(pltpu.VMEM), whole(pltpu.VMEM), whole(pltpu.SMEM)),
        scratch_shapes=[
            pltpu.SMEM((UBLK * IBLK,), jnp.int32),
            pltpu.VMEM((UBLK * EDGE, RANK), jnp.float32),
            pltpu.VMEM((MAXB, EDGE, EDGE), jnp.bfloat16),
            pltpu.SemaphoreType.DMA((MAXB // CHUNK,)),
            pltpu.SemaphoreType.DMA,
        ],
        compiler_params=grant(16),
        name="user_pass",
    )(slots, count, users, gathered, values)


def item_pass(core, places, users, items, values, share):
    ranks = items.shape[0] // (2 * share)
    return pl.pallas_call(
        item_kernel,
        out_shape=(
            jax.ShapeDtypeStruct((ranks, share, RANK), jnp.float32),
            jax.ShapeDtypeStruct((ranks, share, RANK), jnp.bfloat16),
        ),
        in_specs=[
            whole(pltpu.SMEM),
            whole(pltpu.SMEM),
            whole(pltpu.VMEM),
            whole(pltpu.VMEM),
            whole(pltpu.HBM),
        ],
        out_specs=(whole(pltpu.VMEM), whole(pltpu.VMEM)),
        scratch_shapes=[
            pltpu.VMEM((RANK, UBLK * EDGE), jnp.bfloat16),
            pltpu.VMEM((MAXB, EDGE, EDGE), jnp.bfloat16),
            pltpu.SemaphoreType.DMA((MAXB // CHUNK,)),
        ],
        compiler_params=grant(16),
        name="item_pass",
    )(core, places, users, items, values)


def user_update(offset, got, parameter, first, second, scale):
    share = jax.ShapeDtypeStruct((EDGE, RANK), jnp.float32)
    return pl.pallas_call(
        functools.partial(user_update_kernel, scale=scale),
        out_shape=(share, share, share, jax.ShapeDtypeStruct(got.shape, jnp.bfloat16)),
        in_specs=[whole(pltpu.SMEM), whole(pltpu.VMEM)] + [whole(pltpu.HBM)] * 3,
        out_specs=(whole(pltpu.VMEM),) * 4,
        scratch_shapes=[
            pltpu.VMEM((3, EDGE, RANK), jnp.float32),
            pltpu.SemaphoreType.DMA((3,)),
        ],
        compiler_params=grant(16),
        name="user_update",
    )(offset, got, parameter, first, second)


def far(array):
    return pltpu.with_memory_space_constraint(array, pltpu.HBM)


def on_device(
    user_factors,
    user_moment_one,
    user_moment_two,
    item_factors,
    item_moment_one,
    item_moment_two,
    block_slot,
    block_count,
    block_values,
):
    slots = block_slot.reshape(MAXB)
    count = block_count.reshape(1)
    values = far(block_values.reshape(MAXB, EDGE, EDGE))
    user_state = [far(array) for array in (user_factors, user_moment_one, user_moment_two)]
    item_total = IBLK * EDGE * lax.axis_size(ITEMS)
    user_total = user_factors.shape[0] * lax.axis_size(USERS)
    shared = share_items(item_factors, lax.axis_size(("z_hi", "y")))
    half = lax.all_to_all(shared, ("z_hi", "y"), 0, 0)
    gathered = lax.all_gather(half, "core", axis=0)
    user_partial, items, places = user_pass(slots, count, user_state[0], gathered, values)
    user_share = user_factors.shape[0] // lax.axis_size(ITEMS)
    user_offset = lax.axis_index(ITEMS) * user_share
    sent = user_partial.reshape(-1, user_share, RANK)
    got = lax.all_to_all(sent, ITEMS, 0, 0)
    new_user, new_user_one, new_user_two, shared = user_update(
        user_offset.reshape(1), got, *user_state, 1.0 / math.sqrt(item_total)
    )
    new_low = lax.all_to_all(shared, ITEMS, 0, 0).reshape(-1, RANK)
    core = lax.axis_index("core").reshape(1)
    keep, sent = item_pass(core, places, new_low, items, values, item_factors.shape[0])
    other = lax.ppermute(sent, "core", [(0, 1), (1, 0)])
    both = (keep + other.astype(jnp.float32)).astype(jnp.bfloat16)
    got = lax.all_to_all(both, ("z_hi", "y"), 0, 0)
    item_sum = jnp.sum(got.astype(jnp.float32), axis=0)
    new_item, new_item_one, new_item_two = adam_update(
        item_factors, item_moment_one, item_moment_two, item_sum, 1.0 / math.sqrt(user_total)
    )
    return (new_user, new_user_one, new_user_two, new_item, new_item_one, new_item_two)


def solution(mesh):
    fine = Mesh(mesh.devices.reshape(3, 8, 2, 4, 4), PARTS)
    return jax.shard_map(
        on_device,
        mesh=fine,
        in_specs=(
            P(USERS, None),
            P(USERS, None),
            P(USERS, None),
            P(ITEMS + USERS, None),
            P(ITEMS + USERS, None),
            P(ITEMS + USERS, None),
            P(USERS, ITEMS, None),
            P(USERS, ITEMS),
            P(USERS, ITEMS, None, None, None),
        ),
        out_specs=(
            P(USERS + ITEMS, None),
            P(USERS + ITEMS, None),
            P(USERS + ITEMS, None),
            P(ITEMS + USERS, None),
            P(ITEMS + USERS, None),
            P(ITEMS + USERS, None),
        ),
        check_vma=False,
    )
```

```python
import functools
import math

import jax
import jax.numpy as jnp
from jax import lax
from jax.experimental import pallas as pl
from jax.experimental.pallas import tpu as pltpu
from jax.sharding import Mesh
from jax.sharding import PartitionSpec as P

conf_alpha = 0.5
reg_weight = 0.5
beta_one = 0.9
beta_two = 0.95
learn_rate = 0.1
adam_eps = 1e-08
correction_one = 1.0 - beta_one**11
correction_two = 1.0 - beta_two**11

EDGE = 128
RANK = 128
UBLK = 16
IBLK = 12
MAXB = 128
CHUNK = 8
USER_PAIRS = 2
ITEM_PAIRS = 2
PARTS = ("z_hi", "y", "core", "x", "z_lo")
USERS = PARTS[:3]
ITEMS = PARTS[3:]


def adam_update(parameter, first_moment, second_moment, grad_sum, grad_scale):
    gradient = grad_sum * grad_scale + reg_weight * parameter
    first_new = beta_one * first_moment + (1.0 - beta_one) * gradient
    second_new = beta_two * second_moment + (1.0 - beta_two) * gradient * gradient
    step_size = first_new / correction_one / (jnp.sqrt(second_new / correction_two) + adam_eps)
    return (parameter - learn_rate * step_size, first_new, second_new)


def dot_nt(left, right):
    return lax.dot_general(
        left, right, (((1,), (1,)), ((), ())), preferred_element_type=jnp.float32
    )


def dot_nn(left, right):
    return lax.dot_general(
        left, right, (((1,), (0,)), ((), ())), preferred_element_type=jnp.float32
    )


def fill_places(count, slots, places):
    for place in range(UBLK * IBLK):
        places[place] = MAXB

    def advance(turn, carry):
        for inner in range(CHUNK):
            listed = turn * CHUNK + inner
            place = slots[listed]
            places[place] = jnp.where(listed < count, listed, places[place])
        return carry

    lax.fori_loop(0, (count + CHUNK - 1) // CHUNK, advance, 0)


def weighted(predicted, place, target):
    live = place < MAXB
    base = jnp.where(live, 1.0, 0.0).astype(jnp.float32)
    slope = jnp.where(live, conf_alpha, 0.0).astype(jnp.float32)
    target = target.astype(jnp.float32)
    return ((base + slope * target) * (predicted - target)).astype(jnp.bfloat16)


def square_error(user_pair, item_pair, pair, turn, places, buffer):
    predicted = dot_nt(user_pair, item_pair)
    rows = []
    for row in range(2):
        columns = []
        for column in range(2):
            part = predicted[row * EDGE : (row + 1) * EDGE, column * EDGE : (column + 1) * EDGE]
            block, item = pair * 2 + row, turn * 2 + column
            columns.append(weighted(part, places[block * IBLK + item], buffer[block, item]))
        rows.append(jnp.concatenate(columns, axis=1))
    return jnp.concatenate(rows, axis=0)


def open_kernel(slots, count, users, values, low, places_out, dense, places, arrivals):
    fill_places(count[0], slots, places)

    def send(block, carry):
        for item in range(IBLK):
            place = jnp.minimum(places[block * IBLK + item], MAXB - 1)
            pltpu.make_async_copy(
                values.at[place], dense.at[block, item], arrivals.at[block]
            ).start()
        return carry

    lax.fori_loop(0, UBLK, send, 0)
    low[...] = users[...].astype(jnp.bfloat16)
    for place in range(UBLK * IBLK):
        places_out[place] = places[place]
    for block in range(UBLK):
        pltpu.make_async_copy(
            values.at[pl.ds(0, IBLK)], dense.at[block], arrivals.at[block]
        ).wait()


def user_kernel(places, users, gathered, dense, out, panel, turned, buffer, arrivals):
    def arrival(pair):
        rows = pl.ds(pair * 2, 2)
        return pltpu.make_async_copy(dense.at[rows], buffer.at[rows], arrivals.at[pair])

    for pair in range(UBLK // 2):
        arrival(pair).start()
    share = gathered.shape[2]
    for rank in range(gathered.shape[1]):
        for core in range(2):
            first = (rank * 2 + core) * share
            panel[first : first + share, :] = gathered[core, rank]
    for block in range(IBLK):
        span = slice(block * EDGE, (block + 1) * EDGE)
        turned[:, span] = panel[span, :].T

    def advance(step, carry):
        for part in range(USER_PAIRS):
            arrival(step * USER_PAIRS + part).wait()
        for part in range(USER_PAIRS):
            pair = step * USER_PAIRS + part
            rows = pl.ds(pl.multiple_of(pair * 2 * EDGE, 2 * EDGE), 2 * EDGE)
            user_pair = users[rows, :]
            errors = []
            for turn in range(IBLK // 2):
                item_pair = panel[turn * 2 * EDGE : (turn + 1) * 2 * EDGE, :]
                errors.append(square_error(user_pair, item_pair, pair, turn, places, buffer))
            total = dot_nt(turned[...], jnp.concatenate(errors, axis=1))
            out[rows, :] = total.T.astype(jnp.bfloat16)
        return carry

    lax.fori_loop(0, UBLK // 2 // USER_PAIRS, advance, 0)


def item_kernel(core, places, users, items, dense, keep, sent, turned, buffer, arrivals):
    def arrival(turn):
        columns = pl.ds(turn * 2, 2)
        return pltpu.make_async_copy(
            dense.at[:, columns], buffer.at[:, columns], arrivals.at[turn]
        )

    for turn in range(IBLK // 2):
        arrival(turn).start()
    for block in range(UBLK):
        turned[:, block * EDGE : (block + 1) * EDGE] = users[
            block * EDGE : (block + 1) * EDGE, :
        ].T
    share = keep.shape[1]
    ranks = EDGE // share
    first_core = core[0] == 0

    def advance(step, carry):
        for part in range(ITEM_PAIRS):
            arrival(step * ITEM_PAIRS + part).wait()
        for part in range(ITEM_PAIRS):
            turn = step * ITEM_PAIRS + part
            rows = pl.ds(pl.multiple_of(turn * 2 * EDGE, 2 * EDGE), 2 * EDGE)
            item_pair = items[rows, :]
            errors = []
            for pair in range(UBLK // 2):
                span = slice(pair * 2 * EDGE, (pair + 1) * 2 * EDGE)
                errors.append(square_error(users[span, :], item_pair, pair, turn, places, buffer))
            running = dot_nn(turned[...], jnp.concatenate(errors, axis=0))
            split = running.T.reshape(ranks, 2, share, RANK)
            even, odd = split[:, 0], split[:, 1]
            where = pl.ds(turn * ranks, ranks)
            keep[where] = jnp.where(first_core, even, odd)
            sent[where] = jnp.where(first_core, odd, even).astype(jnp.bfloat16)
        return carry

    lax.fori_loop(0, IBLK // 2 // ITEM_PAIRS, advance, 0)


def user_update_kernel(
    offset, got, parameter, first, second, new, new_first, new_second, shared, mine, arrivals, scale
):
    rows = pl.ds(pl.multiple_of(offset[0], EDGE), EDGE)
    copies = [
        pltpu.make_async_copy(source.at[rows], mine.at[place], arrivals.at[place])
        for place, source in enumerate((parameter, first, second))
    ]
    for copy in copies:
        copy.start()
    total = got[0].astype(jnp.float32)
    for rank in range(1, got.shape[0]):
        total = total + got[rank].astype(jnp.float32)
    for copy in copies:
        copy.wait()
    updated = adam_update(mine[0], mine[1], mine[2], total, scale)
    new[...], new_first[...], new_second[...] = updated
    low = updated[0].astype(jnp.bfloat16)
    for rank in range(got.shape[0]):
        shared[rank] = low


def share_kernel(items, shared):
    low = items[...].astype(jnp.bfloat16)
    for rank in range(shared.shape[0]):
        shared[rank] = low


def whole(space):
    return pl.BlockSpec(memory_space=space)


def grant(mebibytes):
    return pltpu.CompilerParams(vmem_limit_bytes=mebibytes * 1024 * 1024)


def share_items(items, ranks):
    return pl.pallas_call(
        share_kernel,
        out_shape=jax.ShapeDtypeStruct((ranks,) + items.shape, jnp.bfloat16),
        in_specs=[whole(pltpu.VMEM)],
        out_specs=whole(pltpu.VMEM),
        name="share_items",
    )(items)


SCALAR = whole(pltpu.SMEM)
VECTOR = whole(pltpu.VMEM)
DISTANT = whole(pltpu.HBM)


def open_pass(slots, count, users, values):
    return pl.pallas_call(
        open_kernel,
        out_shape=(
            jax.ShapeDtypeStruct((UBLK * EDGE, RANK), jnp.bfloat16),
            jax.ShapeDtypeStruct((UBLK * IBLK,), jnp.int32),
            jax.ShapeDtypeStruct((UBLK, IBLK, EDGE, EDGE), jnp.bfloat16),
        ),
        in_specs=[SCALAR, SCALAR, VECTOR, DISTANT],
        out_specs=(VECTOR, SCALAR, DISTANT),
        scratch_shapes=[
            pltpu.SMEM((UBLK * IBLK,), jnp.int32),
            pltpu.SemaphoreType.DMA((UBLK,)),
        ],
        name="open_pass",
    )(slots, count, users, values)


def user_pass(places, users, gathered, dense):
    panel = (gathered.shape[0] * gathered.shape[1] * gathered.shape[2], RANK)
    return pl.pallas_call(
        user_kernel,
        out_shape=(
            jax.ShapeDtypeStruct((UBLK * EDGE, RANK), jnp.bfloat16),
            jax.ShapeDtypeStruct(panel, jnp.bfloat16),
        ),
        in_specs=[SCALAR, VECTOR, VECTOR, DISTANT],
        out_specs=(VECTOR, VECTOR),
        scratch_shapes=[
            pltpu.VMEM((RANK, IBLK * EDGE), jnp.bfloat16),
            pltpu.VMEM((UBLK, IBLK, EDGE, EDGE), jnp.bfloat16),
            pltpu.SemaphoreType.DMA((UBLK // 2,)),
        ],
        compiler_params=grant(20),
        name="user_pass",
    )(places, users, gathered, dense)


def item_pass(core, places, users, items, dense, share):
    ranks = items.shape[0] // (2 * share)
    return pl.pallas_call(
        item_kernel,
        out_shape=(
            jax.ShapeDtypeStruct((ranks, share, RANK), jnp.float32),
            jax.ShapeDtypeStruct((ranks, share, RANK), jnp.bfloat16),
        ),
        in_specs=[SCALAR, SCALAR, VECTOR, VECTOR, DISTANT],
        out_specs=(VECTOR, VECTOR),
        scratch_shapes=[
            pltpu.VMEM((RANK, UBLK * EDGE), jnp.bfloat16),
            pltpu.VMEM((UBLK, IBLK, EDGE, EDGE), jnp.bfloat16),
            pltpu.SemaphoreType.DMA((IBLK // 2,)),
        ],
        compiler_params=grant(20),
        name="item_pass",
    )(core, places, users, items, dense)


def user_update(offset, got, parameter, first, second, scale):
    share = jax.ShapeDtypeStruct((EDGE, RANK), jnp.float32)
    return pl.pallas_call(
        functools.partial(user_update_kernel, scale=scale),
        out_shape=(share, share, share, jax.ShapeDtypeStruct(got.shape, jnp.bfloat16)),
        in_specs=[whole(pltpu.SMEM), whole(pltpu.VMEM)] + [whole(pltpu.HBM)] * 3,
        out_specs=(whole(pltpu.VMEM),) * 4,
        scratch_shapes=[
            pltpu.VMEM((3, EDGE, RANK), jnp.float32),
            pltpu.SemaphoreType.DMA((3,)),
        ],
        compiler_params=grant(16),
        name="user_update",
    )(offset, got, parameter, first, second)


def far(array):
    return pltpu.with_memory_space_constraint(array, pltpu.HBM)


def on_device(
    user_factors,
    user_moment_one,
    user_moment_two,
    item_factors,
    item_moment_one,
    item_moment_two,
    block_slot,
    block_count,
    block_values,
):
    slots = far(block_slot.reshape(MAXB))
    count = block_count.reshape(1)
    values = far(block_values.reshape(MAXB, EDGE, EDGE))
    user_state = [far(array) for array in (user_factors, user_moment_one, user_moment_two)]
    item_total = IBLK * EDGE * lax.axis_size(ITEMS)
    user_total = user_factors.shape[0] * lax.axis_size(USERS)
    shared = share_items(item_factors, lax.axis_size(("z_hi", "y")))
    half = lax.all_to_all(shared, ("z_hi", "y"), 0, 0)
    user_low, places, dense = open_pass(slots, count, user_factors, values)
    gathered = lax.all_gather(half, "core", axis=0)
    user_partial, items = user_pass(far(places), far(user_low), gathered, far(dense))
    user_share = user_factors.shape[0] // lax.axis_size(ITEMS)
    user_offset = lax.axis_index(ITEMS) * user_share
    sent = user_partial.reshape(-1, user_share, RANK)
    got = lax.all_to_all(sent, ITEMS, 0, 0)
    new_user, new_user_one, new_user_two, shared = user_update(
        user_offset.reshape(1), got, *user_state, 1.0 / math.sqrt(item_total)
    )
    new_low = lax.all_to_all(shared, ITEMS, 0, 0).reshape(-1, RANK)
    core = lax.axis_index("core").reshape(1)
    keep, sent = item_pass(core, far(places), new_low, items, far(dense), item_factors.shape[0])
    other = lax.ppermute(sent, "core", [(0, 1), (1, 0)])
    both = (keep + other.astype(jnp.float32)).astype(jnp.bfloat16)
    got = lax.all_to_all(both, ("z_hi", "y"), 0, 0)
    item_sum = jnp.sum(got.astype(jnp.float32), axis=0)
    new_item, new_item_one, new_item_two = adam_update(
        item_factors, item_moment_one, item_moment_two, item_sum, 1.0 / math.sqrt(user_total)
    )
    return (new_user, new_user_one, new_user_two, new_item, new_item_one, new_item_two)


def solution(mesh):
    fine = Mesh(mesh.devices.reshape(3, 8, 2, 4, 4), PARTS)
    return jax.shard_map(
        on_device,
        mesh=fine,
        in_specs=(
            P(USERS, None),
            P(USERS, None),
            P(USERS, None),
            P(ITEMS + USERS, None),
            P(ITEMS + USERS, None),
            P(ITEMS + USERS, None),
            P(USERS, ITEMS, None),
            P(USERS, ITEMS),
            P(USERS, ITEMS, None, None, None),
        ),
        out_specs=(
            P(USERS + ITEMS, None),
            P(USERS + ITEMS, None),
            P(USERS + ITEMS, None),
            P(ITEMS + USERS, None),
            P(ITEMS + USERS, None),
            P(ITEMS + USERS, None),
        ),
        check_vma=False,
    )
```

```python
import functools
import math

import jax
import jax.numpy as jnp
from jax import lax
from jax.experimental import pallas as pl
from jax.experimental.pallas import tpu as pltpu
from jax.sharding import Mesh
from jax.sharding import PartitionSpec as P

conf_alpha = 0.5
reg_weight = 0.5
beta_one = 0.9
beta_two = 0.95
learn_rate = 0.1
adam_eps = 1e-08
correction_one = 1.0 - beta_one**11
correction_two = 1.0 - beta_two**11

EDGE = 128
RANK = 128
UBLK = 16
IBLK = 12
MAXB = 128
CHUNK = 8
USER_PAIRS = 2
ITEM_PAIRS = 2
PARTS = ("z_hi", "y", "core", "x", "z_lo")
USERS = PARTS[:3]
ITEMS = PARTS[3:]


def adam_update(parameter, first_moment, second_moment, grad_sum, grad_scale):
    gradient = grad_sum * grad_scale + reg_weight * parameter
    first_new = beta_one * first_moment + (1.0 - beta_one) * gradient
    second_new = beta_two * second_moment + (1.0 - beta_two) * gradient * gradient
    step_size = first_new / correction_one / (jnp.sqrt(second_new / correction_two) + adam_eps)
    return (parameter - learn_rate * step_size, first_new, second_new)


def dot_nt(left, right):
    return lax.dot_general(
        left, right, (((1,), (1,)), ((), ())), preferred_element_type=jnp.float32
    )


def dot_nn(left, right):
    return lax.dot_general(
        left, right, (((1,), (0,)), ((), ())), preferred_element_type=jnp.float32
    )


def fill_places(count, slots, places):
    for place in range(UBLK * IBLK):
        places[place] = MAXB

    def advance(turn, carry):
        for inner in range(CHUNK):
            listed = turn * CHUNK + inner
            place = slots[listed]
            places[place] = jnp.where(listed < count, listed, places[place])
        return carry

    lax.fori_loop(0, (count + CHUNK - 1) // CHUNK, advance, 0)


def weighted(predicted, place, target):
    live = place < MAXB
    base = jnp.where(live, 1.0, 0.0).astype(jnp.float32)
    slope = jnp.where(live, conf_alpha, 0.0).astype(jnp.float32)
    target = target.astype(jnp.float32)
    return ((base + slope * target) * (predicted - target)).astype(jnp.bfloat16)


def square_error(user_pair, item_pair, pair, turn, places, buffer):
    predicted = dot_nt(user_pair, item_pair)
    rows = []
    for row in range(2):
        columns = []
        for column in range(2):
            part = predicted[row * EDGE : (row + 1) * EDGE, column * EDGE : (column + 1) * EDGE]
            block, item = pair * 2 + row, turn * 2 + column
            columns.append(weighted(part, places[block * IBLK + item], buffer[block, item]))
        rows.append(jnp.concatenate(columns, axis=1))
    return jnp.concatenate(rows, axis=0)


def open_kernel(slots, count, users, values, low, places_out, dense, places, arrivals):
    fill_places(count[0], slots, places)

    def send(block, carry):
        for item in range(IBLK):
            place = jnp.minimum(places[block * IBLK + item], MAXB - 1)
            pltpu.make_async_copy(
                values.at[place], dense.at[block, item], arrivals.at[block]
            ).start()
        return carry

    lax.fori_loop(0, UBLK, send, 0)
    low[...] = users[...].astype(jnp.bfloat16)
    for place in range(UBLK * IBLK):
        places_out[place] = places[place]
    for block in range(UBLK):
        pltpu.make_async_copy(
            values.at[pl.ds(0, IBLK)], dense.at[block], arrivals.at[block]
        ).wait()


def user_kernel(places, users, gathered, dense, out, panel, buffer, arrivals):
    def arrival(pair):
        rows = pl.ds(pair * 2, 2)
        return pltpu.make_async_copy(dense.at[rows], buffer.at[rows], arrivals.at[pair])

    for pair in range(UBLK // 2):
        arrival(pair).start()
    share = gathered.shape[2]
    for rank in range(gathered.shape[1]):
        for core in range(2):
            first = (rank * 2 + core) * share
            panel[first : first + share, :] = gathered[core, rank]

    def advance(step, carry):
        for part in range(USER_PAIRS):
            arrival(step * USER_PAIRS + part).wait()
        for part in range(USER_PAIRS):
            pair = step * USER_PAIRS + part
            rows = pl.ds(pl.multiple_of(pair * 2 * EDGE, 2 * EDGE), 2 * EDGE)
            user_pair = users[rows, :]
            errors = []
            for turn in range(IBLK // 2):
                item_pair = panel[turn * 2 * EDGE : (turn + 1) * 2 * EDGE, :]
                errors.append(square_error(user_pair, item_pair, pair, turn, places, buffer))
            total = dot_nn(jnp.concatenate(errors, axis=1), panel[...])
            out[rows, :] = total.astype(jnp.bfloat16)
        return carry

    lax.fori_loop(0, UBLK // 2 // USER_PAIRS, advance, 0)


def item_kernel(core, places, users, items, dense, keep, sent, turned, buffer, arrivals):
    def arrival(turn):
        columns = pl.ds(turn * 2, 2)
        return pltpu.make_async_copy(
            dense.at[:, columns], buffer.at[:, columns], arrivals.at[turn]
        )

    for turn in range(IBLK // 2):
        arrival(turn).start()
    for block in range(UBLK):
        turned[:, block * EDGE : (block + 1) * EDGE] = users[
            block * EDGE : (block + 1) * EDGE, :
        ].T
    share = keep.shape[1]
    ranks = EDGE // share
    first_core = core[0] == 0

    def advance(step, carry):
        for part in range(ITEM_PAIRS):
            arrival(step * ITEM_PAIRS + part).wait()
        for part in range(ITEM_PAIRS):
            turn = step * ITEM_PAIRS + part
            rows = pl.ds(pl.multiple_of(turn * 2 * EDGE, 2 * EDGE), 2 * EDGE)
            item_pair = items[rows, :]
            errors = []
            for pair in range(UBLK // 2):
                span = slice(pair * 2 * EDGE, (pair + 1) * 2 * EDGE)
                errors.append(square_error(users[span, :], item_pair, pair, turn, places, buffer))
            running = dot_nn(turned[...], jnp.concatenate(errors, axis=0))
            split = running.T.reshape(ranks, 2, share, RANK)
            even, odd = split[:, 0], split[:, 1]
            where = pl.ds(turn * ranks, ranks)
            keep[where] = jnp.where(first_core, even, odd)
            sent[where] = jnp.where(first_core, odd, even).astype(jnp.bfloat16)
        return carry

    lax.fori_loop(0, IBLK // 2 // ITEM_PAIRS, advance, 0)


def user_update_kernel(
    offset, got, parameter, first, second, new, new_first, new_second, shared, mine, arrivals, scale
):
    rows = pl.ds(pl.multiple_of(offset[0], EDGE), EDGE)
    copies = [
        pltpu.make_async_copy(source.at[rows], mine.at[place], arrivals.at[place])
        for place, source in enumerate((parameter, first, second))
    ]
    for copy in copies:
        copy.start()
    total = got[0].astype(jnp.float32)
    for rank in range(1, got.shape[0]):
        total = total + got[rank].astype(jnp.float32)
    for copy in copies:
        copy.wait()
    updated = adam_update(mine[0], mine[1], mine[2], total, scale)
    new[...], new_first[...], new_second[...] = updated
    low = updated[0].astype(jnp.bfloat16)
    for rank in range(got.shape[0]):
        shared[rank] = low


def share_kernel(items, shared):
    low = items[...].astype(jnp.bfloat16)
    for rank in range(shared.shape[0]):
        shared[rank] = low


def whole(space):
    return pl.BlockSpec(memory_space=space)


def grant(mebibytes):
    return pltpu.CompilerParams(vmem_limit_bytes=mebibytes * 1024 * 1024)


def share_items(items, ranks):
    return pl.pallas_call(
        share_kernel,
        out_shape=jax.ShapeDtypeStruct((ranks,) + items.shape, jnp.bfloat16),
        in_specs=[whole(pltpu.VMEM)],
        out_specs=whole(pltpu.VMEM),
        name="share_items",
    )(items)


SCALAR = whole(pltpu.SMEM)
VECTOR = whole(pltpu.VMEM)
DISTANT = whole(pltpu.HBM)


def open_pass(slots, count, users, values):
    return pl.pallas_call(
        open_kernel,
        out_shape=(
            jax.ShapeDtypeStruct((UBLK * EDGE, RANK), jnp.bfloat16),
            jax.ShapeDtypeStruct((UBLK * IBLK,), jnp.int32),
            jax.ShapeDtypeStruct((UBLK, IBLK, EDGE, EDGE), jnp.bfloat16),
        ),
        in_specs=[SCALAR, SCALAR, VECTOR, DISTANT],
        out_specs=(VECTOR, SCALAR, VECTOR),
        scratch_shapes=[
            pltpu.SMEM((UBLK * IBLK,), jnp.int32),
            pltpu.SemaphoreType.DMA((UBLK,)),
        ],
        name="open_pass",
    )(slots, count, users, values)


def user_pass(places, users, gathered, dense):
    panel = (gathered.shape[0] * gathered.shape[1] * gathered.shape[2], RANK)
    return pl.pallas_call(
        user_kernel,
        out_shape=(
            jax.ShapeDtypeStruct((UBLK * EDGE, RANK), jnp.bfloat16),
            jax.ShapeDtypeStruct(panel, jnp.bfloat16),
        ),
        in_specs=[SCALAR, VECTOR, VECTOR, DISTANT],
        out_specs=(VECTOR, VECTOR),
        scratch_shapes=[
            pltpu.VMEM((UBLK, IBLK, EDGE, EDGE), jnp.bfloat16),
            pltpu.SemaphoreType.DMA((UBLK // 2,)),
        ],
        compiler_params=grant(20),
        name="user_pass",
    )(places, users, gathered, dense)


def item_pass(core, places, users, items, dense, share):
    ranks = items.shape[0] // (2 * share)
    return pl.pallas_call(
        item_kernel,
        out_shape=(
            jax.ShapeDtypeStruct((ranks, share, RANK), jnp.float32),
            jax.ShapeDtypeStruct((ranks, share, RANK), jnp.bfloat16),
        ),
        in_specs=[SCALAR, SCALAR, VECTOR, VECTOR, DISTANT],
        out_specs=(VECTOR, VECTOR),
        scratch_shapes=[
            pltpu.VMEM((RANK, UBLK * EDGE), jnp.bfloat16),
            pltpu.VMEM((UBLK, IBLK, EDGE, EDGE), jnp.bfloat16),
            pltpu.SemaphoreType.DMA((IBLK // 2,)),
        ],
        compiler_params=grant(20),
        name="item_pass",
    )(core, places, users, items, dense)


def user_update(offset, got, parameter, first, second, scale):
    share = jax.ShapeDtypeStruct((EDGE, RANK), jnp.float32)
    return pl.pallas_call(
        functools.partial(user_update_kernel, scale=scale),
        out_shape=(share, share, share, jax.ShapeDtypeStruct(got.shape, jnp.bfloat16)),
        in_specs=[whole(pltpu.SMEM), whole(pltpu.VMEM)] + [whole(pltpu.HBM)] * 3,
        out_specs=(whole(pltpu.VMEM),) * 4,
        scratch_shapes=[
            pltpu.VMEM((3, EDGE, RANK), jnp.float32),
            pltpu.SemaphoreType.DMA((3,)),
        ],
        compiler_params=grant(16),
        name="user_update",
    )(offset, got, parameter, first, second)


def far(array):
    return pltpu.with_memory_space_constraint(array, pltpu.HBM)


def on_device(
    user_factors,
    user_moment_one,
    user_moment_two,
    item_factors,
    item_moment_one,
    item_moment_two,
    block_slot,
    block_count,
    block_values,
):
    slots = far(block_slot.reshape(MAXB))
    count = block_count.reshape(1)
    values = far(block_values.reshape(MAXB, EDGE, EDGE))
    user_state = [far(array) for array in (user_factors, user_moment_one, user_moment_two)]
    item_total = IBLK * EDGE * lax.axis_size(ITEMS)
    user_total = user_factors.shape[0] * lax.axis_size(USERS)
    shared = share_items(item_factors, lax.axis_size(("z_hi", "y")))
    half = lax.all_to_all(shared, ("z_hi", "y"), 0, 0)
    user_low, places, dense = open_pass(slots, count, user_factors, values)
    gathered = lax.all_gather(half, "core", axis=0)
    user_partial, items = user_pass(far(places), far(user_low), gathered, far(dense))
    user_share = user_factors.shape[0] // lax.axis_size(ITEMS)
    user_offset = lax.axis_index(ITEMS) * user_share
    sent = user_partial.reshape(-1, user_share, RANK)
    got = lax.all_to_all(sent, ITEMS, 0, 0)
    new_user, new_user_one, new_user_two, shared = user_update(
        user_offset.reshape(1), got, *user_state, 1.0 / math.sqrt(item_total)
    )
    new_low = lax.all_to_all(shared, ITEMS, 0, 0).reshape(-1, RANK)
    core = lax.axis_index("core").reshape(1)
    keep, sent = item_pass(core, far(places), new_low, items, far(dense), item_factors.shape[0])
    other = lax.ppermute(sent, "core", [(0, 1), (1, 0)])
    both = (keep + other.astype(jnp.float32)).astype(jnp.bfloat16)
    got = lax.all_to_all(both, ("z_hi", "y"), 0, 0)
    item_sum = jnp.sum(got.astype(jnp.float32), axis=0)
    new_item, new_item_one, new_item_two = adam_update(
        item_factors, item_moment_one, item_moment_two, item_sum, 1.0 / math.sqrt(user_total)
    )
    return (new_user, new_user_one, new_user_two, new_item, new_item_one, new_item_two)


def solution(mesh):
    fine = Mesh(mesh.devices.reshape(3, 8, 2, 4, 4), PARTS)
    return jax.shard_map(
        on_device,
        mesh=fine,
        in_specs=(
            P(USERS, None),
            P(USERS, None),
            P(USERS, None),
            P(ITEMS + USERS, None),
            P(ITEMS + USERS, None),
            P(ITEMS + USERS, None),
            P(USERS, ITEMS, None),
            P(USERS, ITEMS),
            P(USERS, ITEMS, None, None, None),
        ),
        out_specs=(
            P(USERS + ITEMS, None),
            P(USERS + ITEMS, None),
            P(USERS + ITEMS, None),
            P(ITEMS + USERS, None),
            P(ITEMS + USERS, None),
            P(ITEMS + USERS, None),
        ),
        check_vma=False,
    )
```

```python
import functools
import math

import jax
import jax.numpy as jnp
from jax import lax
from jax.experimental import pallas as pl
from jax.experimental.pallas import tpu as pltpu
from jax.sharding import Mesh
from jax.sharding import PartitionSpec as P

conf_alpha = 0.5
reg_weight = 0.5
beta_one = 0.9
beta_two = 0.95
learn_rate = 0.1
adam_eps = 1e-08
correction_one = 1.0 - beta_one**11
correction_two = 1.0 - beta_two**11

EDGE = 128
RANK = 128
UBLK = 16
IBLK = 12
MAXB = 128
CHUNK = 8
PARTS = ("z_hi", "y", "core", "x", "z_lo")
USERS = PARTS[:3]
ITEMS = PARTS[3:]


def adam_update(parameter, first_moment, second_moment, grad_sum, grad_scale):
    gradient = grad_sum * grad_scale + reg_weight * parameter
    first_new = beta_one * first_moment + (1.0 - beta_one) * gradient
    second_new = beta_two * second_moment + (1.0 - beta_two) * gradient * gradient
    step_size = first_new / correction_one / (jnp.sqrt(second_new / correction_two) + adam_eps)
    return (parameter - learn_rate * step_size, first_new, second_new)


def dot_nt(left, right):
    return lax.dot_general(
        left, right, (((1,), (1,)), ((), ())), preferred_element_type=jnp.float32
    )


def dot_nn(left, right):
    return lax.dot_general(
        left, right, (((1,), (0,)), ((), ())), preferred_element_type=jnp.float32
    )


def fill_places(count, slots, places):
    for place in range(UBLK * IBLK):
        places[place] = MAXB

    def advance(turn, carry):
        for inner in range(CHUNK):
            listed = turn * CHUNK + inner
            place = slots[listed]
            places[place] = jnp.where(listed < count, listed, places[place])
        return carry

    lax.fori_loop(0, (count + CHUNK - 1) // CHUNK, advance, 0)


def value_copies(values, buffer, arrivals):
    return [
        pltpu.make_async_copy(
            values.at[pl.ds(chunk * CHUNK, CHUNK)],
            buffer.at[pl.ds(chunk * CHUNK, CHUNK)],
            arrivals.at[chunk],
        )
        for chunk in range(MAXB // CHUNK)
    ]


def weighted(predicted, place, values):
    live = place < MAXB
    base = jnp.where(live, 1.0, 0.0).astype(jnp.float32)
    slope = jnp.where(live, conf_alpha, 0.0).astype(jnp.float32)
    target = values[jnp.minimum(place, MAXB - 1)].astype(jnp.float32)
    return ((base + slope * target) * (predicted - target)).astype(jnp.bfloat16)


def square_error(user_pair, item_pair, first_place, places, values):
    predicted = dot_nt(user_pair, item_pair)
    rows = []
    for row in range(2):
        columns = []
        for column in range(2):
            part = predicted[row * EDGE : (row + 1) * EDGE, column * EDGE : (column + 1) * EDGE]
            columns.append(weighted(part, places[first_place + row * IBLK + column], values))
        rows.append(jnp.concatenate(columns, axis=1))
    return jnp.concatenate(rows, axis=0)


def user_kernel(
    slots, count, users, gathered, values, out, panel, places_out, places, low, buffer, arrivals, ready
):
    copies = value_copies(values, buffer, arrivals)
    fetch = pltpu.make_async_copy(users, low, ready)
    fetch.start()
    for copy in copies:
        copy.start()
    fill_places(count[0], slots, places)
    share = gathered.shape[2]
    for rank in range(gathered.shape[1]):
        for core in range(2):
            first = (rank * 2 + core) * share
            panel[first : first + share, :] = gathered[core, rank]
    for place in range(UBLK * IBLK):
        places_out[place] = places[place]
    fetch.wait()
    for copy in copies:
        copy.wait()

    def advance(pair, carry):
        rows = pl.ds(pl.multiple_of(pair * 2 * EDGE, 2 * EDGE), 2 * EDGE)
        user_pair = low[rows, :].astype(jnp.bfloat16)
        errors = []
        for turn in range(IBLK // 2):
            item_pair = panel[turn * 2 * EDGE : (turn + 1) * 2 * EDGE, :]
            errors.append(
                square_error(user_pair, item_pair, pair * 2 * IBLK + turn * 2, places, buffer)
            )
        total = dot_nn(jnp.concatenate(errors, axis=1), panel[...])
        out[rows, :] = total.astype(jnp.bfloat16)
        return carry

    lax.fori_loop(0, UBLK // 2, advance, 0, unroll=4)


def item_kernel(core, places, users, items, values, keep, sent, turned, buffer, arrivals):
    copies = value_copies(values, buffer, arrivals)
    for copy in copies:
        copy.start()
    for block in range(UBLK):
        turned[:, block * EDGE : (block + 1) * EDGE] = users[
            block * EDGE : (block + 1) * EDGE, :
        ].T
    share = keep.shape[1]
    ranks = EDGE // share
    first_core = core[0] == 0
    for copy in copies:
        copy.wait()

    def advance(turn, carry):
        rows = pl.ds(pl.multiple_of(turn * 2 * EDGE, 2 * EDGE), 2 * EDGE)
        item_pair = items[rows, :]
        errors = []
        for pair in range(UBLK // 2):
            span = slice(pair * 2 * EDGE, (pair + 1) * 2 * EDGE)
            errors.append(
                square_error(users[span, :], item_pair, pair * 2 * IBLK + turn * 2, places, buffer)
            )
        running = dot_nn(turned[...], jnp.concatenate(errors, axis=0))
        split = running.T.reshape(ranks, 2, share, RANK)
        even, odd = split[:, 0], split[:, 1]
        where = pl.ds(turn * ranks, ranks)
        keep[where] = jnp.where(first_core, even, odd)
        sent[where] = jnp.where(first_core, odd, even).astype(jnp.bfloat16)
        return carry

    lax.fori_loop(0, IBLK // 2, advance, 0, unroll=3)


def user_update_kernel(
    offset, got, parameter, first, second, new, new_first, new_second, shared, mine, arrivals, scale
):
    rows = pl.ds(pl.multiple_of(offset[0], EDGE), EDGE)
    copies = [
        pltpu.make_async_copy(source.at[rows], mine.at[place], arrivals.at[place])
        for place, source in enumerate((parameter, first, second))
    ]
    for copy in copies:
        copy.start()
    total = got[0].astype(jnp.float32)
    for rank in range(1, got.shape[0]):
        total = total + got[rank].astype(jnp.float32)
    for copy in copies:
        copy.wait()
    updated = adam_update(mine[0], mine[1], mine[2], total, scale)
    new[...], new_first[...], new_second[...] = updated
    low = updated[0].astype(jnp.bfloat16)
    for rank in range(got.shape[0]):
        shared[rank] = low


def share_kernel(items, shared):
    low = items[...].astype(jnp.bfloat16)
    for rank in range(shared.shape[0]):
        shared[rank] = low


def whole(space):
    return pl.BlockSpec(memory_space=space)


def grant(mebibytes):
    return pltpu.CompilerParams(vmem_limit_bytes=mebibytes * 1024 * 1024)


def share_items(items, ranks):
    return pl.pallas_call(
        share_kernel,
        out_shape=jax.ShapeDtypeStruct((ranks,) + items.shape, jnp.bfloat16),
        in_specs=[whole(pltpu.VMEM)],
        out_specs=whole(pltpu.VMEM),
        name="share_items",
    )(items)


def user_pass(slots, count, users, gathered, values):
    panel = (gathered.shape[0] * gathered.shape[1] * gathered.shape[2], RANK)
    return pl.pallas_call(
        user_kernel,
        out_shape=(
            jax.ShapeDtypeStruct((UBLK * EDGE, RANK), jnp.bfloat16),
            jax.ShapeDtypeStruct(panel, jnp.bfloat16),
            jax.ShapeDtypeStruct((UBLK * IBLK,), jnp.int32),
        ),
        in_specs=[
            whole(pltpu.SMEM),
            whole(pltpu.SMEM),
            whole(pltpu.HBM),
            whole(pltpu.VMEM),
            whole(pltpu.HBM),
        ],
        out_specs=(whole(pltpu.VMEM), whole(pltpu.VMEM), whole(pltpu.SMEM)),
        scratch_shapes=[
            pltpu.SMEM((UBLK * IBLK,), jnp.int32),
            pltpu.VMEM((UBLK * EDGE, RANK), jnp.float32),
            pltpu.VMEM((MAXB, EDGE, EDGE), jnp.bfloat16),
            pltpu.SemaphoreType.DMA((MAXB // CHUNK,)),
            pltpu.SemaphoreType.DMA,
        ],
        compiler_params=grant(16),
        name="user_pass",
    )(slots, count, users, gathered, values)


def item_pass(core, places, users, items, values, share):
    ranks = items.shape[0] // (2 * share)
    return pl.pallas_call(
        item_kernel,
        out_shape=(
            jax.ShapeDtypeStruct((ranks, share, RANK), jnp.float32),
            jax.ShapeDtypeStruct((ranks, share, RANK), jnp.bfloat16),
        ),
        in_specs=[
            whole(pltpu.SMEM),
            whole(pltpu.SMEM),
            whole(pltpu.VMEM),
            whole(pltpu.VMEM),
            whole(pltpu.HBM),
        ],
        out_specs=(whole(pltpu.VMEM), whole(pltpu.VMEM)),
        scratch_shapes=[
            pltpu.VMEM((RANK, UBLK * EDGE), jnp.bfloat16),
            pltpu.VMEM((MAXB, EDGE, EDGE), jnp.bfloat16),
            pltpu.SemaphoreType.DMA((MAXB // CHUNK,)),
        ],
        compiler_params=grant(16),
        name="item_pass",
    )(core, places, users, items, values)


def user_update(offset, got, parameter, first, second, scale):
    share = jax.ShapeDtypeStruct((EDGE, RANK), jnp.float32)
    return pl.pallas_call(
        functools.partial(user_update_kernel, scale=scale),
        out_shape=(share, share, share, jax.ShapeDtypeStruct(got.shape, jnp.bfloat16)),
        in_specs=[whole(pltpu.SMEM), whole(pltpu.VMEM)] + [whole(pltpu.HBM)] * 3,
        out_specs=(whole(pltpu.VMEM),) * 4,
        scratch_shapes=[
            pltpu.VMEM((3, EDGE, RANK), jnp.float32),
            pltpu.SemaphoreType.DMA((3,)),
        ],
        compiler_params=grant(16),
        name="user_update",
    )(offset, got, parameter, first, second)


def far(array):
    return pltpu.with_memory_space_constraint(array, pltpu.HBM)


def on_device(
    user_factors,
    user_moment_one,
    user_moment_two,
    item_factors,
    item_moment_one,
    item_moment_two,
    block_slot,
    block_count,
    block_values,
):
    slots = far(block_slot.reshape(MAXB))
    count = block_count.reshape(1)
    values = far(block_values.reshape(MAXB, EDGE, EDGE))
    user_state = [far(array) for array in (user_factors, user_moment_one, user_moment_two)]
    item_total = IBLK * EDGE * lax.axis_size(ITEMS)
    user_total = user_factors.shape[0] * lax.axis_size(USERS)
    shared = share_items(item_factors, lax.axis_size(("z_hi", "y")))
    half = lax.all_to_all(shared, ("z_hi", "y"), 0, 0)
    gathered = lax.all_gather(half, "core", axis=0)
    user_partial, items, places = user_pass(slots, count, user_state[0], gathered, values)
    user_share = user_factors.shape[0] // lax.axis_size(ITEMS)
    user_offset = lax.axis_index(ITEMS) * user_share
    sent = user_partial.reshape(-1, user_share, RANK)
    got = lax.all_to_all(sent, ITEMS, 0, 0)
    new_user, new_user_one, new_user_two, shared = user_update(
        user_offset.reshape(1), got, *user_state, 1.0 / math.sqrt(item_total)
    )
    new_low = lax.all_to_all(shared, ITEMS, 0, 0).reshape(-1, RANK)
    core = lax.axis_index("core").reshape(1)
    keep, sent = item_pass(core, places, new_low, items, values, item_factors.shape[0])
    other = lax.ppermute(sent, "core", [(0, 1), (1, 0)])
    both = (keep + other.astype(jnp.float32)).astype(jnp.bfloat16)
    got = lax.all_to_all(both, ("z_hi", "y"), 0, 0)
    item_sum = jnp.sum(got.astype(jnp.float32), axis=0)
    new_item, new_item_one, new_item_two = adam_update(
        item_factors, item_moment_one, item_moment_two, item_sum, 1.0 / math.sqrt(user_total)
    )
    return (new_user, new_user_one, new_user_two, new_item, new_item_one, new_item_two)


def solution(mesh):
    fine = Mesh(mesh.devices.reshape(3, 8, 2, 4, 4), PARTS)
    return jax.shard_map(
        on_device,
        mesh=fine,
        in_specs=(
            P(USERS, None),
            P(USERS, None),
            P(USERS, None),
            P(ITEMS + USERS, None),
            P(ITEMS + USERS, None),
            P(ITEMS + USERS, None),
            P(USERS, ITEMS, None),
            P(USERS, ITEMS),
            P(USERS, ITEMS, None, None, None),
        ),
        out_specs=(
            P(USERS + ITEMS, None),
            P(USERS + ITEMS, None),
            P(USERS + ITEMS, None),
            P(ITEMS + USERS, None),
            P(ITEMS + USERS, None),
            P(ITEMS + USERS, None),
        ),
        check_vma=False,
    )
```
